32 devices in a mesh: row: 2 (over y), col: 4 (over z), mp: 4 (over x, core).
Axes of the slice: x: 2, y: 2, z: 4, core: 2. Of those that a mesh axis runs over, the one named last changes fastest.
Arguments:
- hidden: bfloat16 [8192, 3584], P(('row', 'col'), 'mp'), may hold values from -6 to 6
- old_logp: float32 [8192], P(('row', 'col')), may hold values from -0.6 to 0.6
- rewards: float32 [64], P(('row', 'col')), may hold values from -4 to 4
- resp_dest: int32 [64], P(('row', 'col')), may hold values from 0 to 7, as said below
- resp_len: int32 [64], P(('row', 'col')), may hold values from 1 to 128, as said below
- resp_offset: int32 [64], P(('row', 'col')), may hold values from 0 to 511, as said below
- prompt_group: int32 [64], P(('row', 'col')), may hold values from 0 to 7, as said below
- attn_gain: bfloat16 [3584], replicated, may hold values from 0.099609375 to 1.8984375
- w_query: bfloat16 [3584, 3584], P(None, 'mp'), may hold values from -0.09375 to 0.09375
- q_bias: bfloat16 [3584], P('mp'), may hold values from -3 to 3
- w_key: bfloat16 [3584, 512], P(None, 'mp'), may hold values from -0.09375 to 0.09375
- k_bias: bfloat16 [512], P('mp'), may hold values from -6 to 6
- w_value: bfloat16 [3584, 512], P(None, 'mp'), may hold values from -0.09375 to 0.09375
- v_bias: bfloat16 [512], P('mp'), may hold values from -3 to 3
- w_out: bfloat16 [3584, 3584], P('mp'), may hold values from -0.5 to 0.5
- final_gain: bfloat16 [3584], replicated, may hold values from 0.099609375 to 1.8984375
- chosen_rows: bfloat16 [4096, 3584], P(('row', 'col', 'mp')), may hold values from -0.01171875 to 0.01171875
- log_normalizer: float32 [4096], P(('row', 'col', 'mp')), may hold values from -0.6 to 0.6
Outputs:
- objective: float32 [4096], P(('row', 'col', 'mp'))
- loss: float32 [], replicated
The draws below stay inside these ranges and needn't reach their ends.
Inputs may be any that keep to these rules, and one draw needn't show every extreme that they name: `resp_dest`: ranks are numbered row index * 4 + col index. A rank's responses go to ranks of the same col index: exactly 4 of them to each such rank, itself included; so every rank receives exactly 8 responses. `resp_len`: the responses bound for one rank hold at most 512 tokens together; in every draw some rank's responses fill all 512 positions, and some response has exactly 128. `resp_offset`: responses bound for one rank lie end to end from position 0, without gaps or intersection. `prompt_group`: each of the 8 groups has exactly 8 responses.
All inputs are finite; a program needn't handle non-finite values.
Results may differ from the reference program's by a relative error of at most 0.0019.
Values may be sent and summed in bfloat16 or wider, within the bound.
A program may use at most 128 MiB of HBM per device.

```python
import jax
import jax.numpy as jnp
from jax import lax

D = 3584
HEADS = 28
KV_HEADS = 4
HEAD = 128
MAXLEN = 128
RESP_DEV = 8
GROUP_SIZE = 8
RANKS = 8
RESPONSES = 64
PACK = 512
N_ROW = 2
N_COL = 4
N_MP = 4


def routing_plan(key):
    base_key = jax.random.fold_in(key, 4242)
    key_list = jax.random.split(base_key, 7)
    per_peer = RESP_DEV // N_ROW
    source_keys = jax.random.split(key_list[0], RANKS)
    shuffles = jax.vmap(lambda one_key: jax.random.permutation(one_key, RESP_DEV))(source_keys)
    source_ids = jnp.arange(RANKS, dtype=jnp.int32)[:, None]
    source_row = source_ids // N_COL
    source_col = source_ids % N_COL
    dest_row = shuffles // per_peer
    slot_in_peer = shuffles % per_peer
    targets = dest_row * N_COL + source_col
    arrival = source_row * per_peer + slot_in_peer
    levels = jax.random.randint(key_list[3], (RANKS, RESP_DEV), 0, 5)
    base_length = jnp.right_shift(jnp.full((RANKS, RESP_DEV), MAXLEN, jnp.int32), levels)
    jitter = jax.random.randint(key_list[4], (RANKS, RESP_DEV), 0, 1 << 20) % (base_length // 4 + 1)
    drawn = jnp.maximum(base_length - jitter, 1)
    chosen_rank = jax.random.randint(key_list[5], (), 0, RANKS)
    chosen_slot = jax.random.randint(key_list[6], (), 0, RESP_DEV - 1)
    extra_slot = (chosen_slot + 1) % (RESP_DEV - 1)
    slot_ids = jnp.arange(RESP_DEV, dtype=jnp.int32)[None, :]
    rank_hit = jnp.arange(RANKS, dtype=jnp.int32)[:, None] == chosen_rank
    rest_tokens = PACK - 1 - MAXLEN
    filler_count = RESP_DEV - 2
    filler = rest_tokens // filler_count
    leftover = rest_tokens % filler_count
    full_row = jnp.where(slot_ids == RESP_DEV - 1, 1, jnp.where(slot_ids == chosen_slot, MAXLEN, filler + jnp.where(slot_ids == extra_slot, leftover, 0)))
    drawn = jnp.where(rank_hit, full_row, drawn).astype(jnp.int32)
    totals = jnp.sum(drawn, 1, keepdims=True)
    lengths = jnp.where(totals > PACK, jnp.maximum(drawn // 2, 1), drawn)
    offsets = jnp.cumsum(lengths, 1) - lengths
    return (targets.reshape(-1).astype(jnp.int32), lengths[targets, arrival].reshape(-1).astype(jnp.int32), offsets[targets, arrival].reshape(-1).astype(jnp.int32))


def draw_resp_dest(key, part):
    return routing_plan(key)[0]


def draw_resp_len(key, part):
    return routing_plan(key)[1]


def draw_resp_offset(key, part):
    return routing_plan(key)[2]


def draw_prompt_group(key, part):
    shuffled = jax.random.permutation(jax.random.fold_in(key, 77), RANKS * RESP_DEV)
    return (shuffled // GROUP_SIZE).astype(jnp.int32)


def steps_of(rng, dims, cuts, smallest, largest):
    def one(axis_at, shards_of):
        draws = jax.random.uniform(jax.random.fold_in(jax.random.fold_in(rng, 6), axis_at), (shards_of,), jnp.float32, smallest / len(cuts), largest / len(cuts))
        return jnp.repeat(jnp.exp(draws), dims[axis_at] // shards_of).reshape((-1,) + (1,) * (len(dims) - axis_at - 1))

    level = one(*cuts[0])
    for cut in cuts[1:]:
        level = level * one(*cut)
    return level


def gaussian(stream_key, shape, scale, limit, shards=(), kind=jnp.bfloat16):
    result = jax.random.normal(stream_key, shape, jnp.float32) * scale
    if len(shards) > 0:
        result = steps_of(stream_key, shape, shards, -0.22, 0.18) * result
    return jnp.clip(result, min=-limit, max=limit).astype(kind)


def setup_inputs(seed: int = 0) -> dict:
    key_of = jax.random.split(jax.random.key(seed), 19)
    return {
        "hidden": gaussian(key_of[0], (RESPONSES * MAXLEN, D), 1.0, 6.0, ((0, 8), (1, 4))),
        "old_logp": gaussian(key_of[1], (RESPONSES * MAXLEN,), 0.1, 0.6, ((0, 8),), jnp.float32),
        "rewards": gaussian(key_of[2], (RESPONSES,), 1.0, 4.0, ((0, 8),), jnp.float32),
        "resp_dest": draw_resp_dest(jax.random.fold_in(key_of[18], 71), 0),
        "resp_len": draw_resp_len(jax.random.fold_in(key_of[18], 71), 0),
        "resp_offset": draw_resp_offset(jax.random.fold_in(key_of[18], 71), 0),
        "prompt_group": draw_prompt_group(jax.random.fold_in(key_of[18], 71), 0),
        "attn_gain": jnp.clip(1.0 + 0.18 * jax.random.normal(key_of[7], (D,), jnp.float32), 0.099609375, 1.8984375).astype(jnp.bfloat16),
        "w_query": gaussian(key_of[8], (D, HEADS * HEAD), D ** -0.5, 0.09375, ((1, 4),)),
        "q_bias": gaussian(key_of[9], (HEADS * HEAD,), 0.5, 3.0, ((0, 4),)),
        "w_key": gaussian(key_of[10], (D, KV_HEADS * HEAD), D ** -0.5, 0.09375, ((1, 4),)),
        "k_bias": gaussian(key_of[11], (KV_HEADS * HEAD,), 1.0, 6.0, ((0, 4),)),
        "w_value": gaussian(key_of[12], (D, KV_HEADS * HEAD), D ** -0.5, 0.09375, ((1, 4),)),
        "v_bias": gaussian(key_of[13], (KV_HEADS * HEAD,), 0.5, 3.0, ((0, 4),)),
        "w_out": gaussian(key_of[14], (HEADS * HEAD, D), HEAD ** -0.5, 0.5, ((0, 4),)),
        "final_gain": jnp.clip(1.0 + 0.18 * jax.random.normal(key_of[15], (D,), jnp.float32), 0.099609375, 1.8984375).astype(jnp.bfloat16),
        "chosen_rows": gaussian(key_of[16], (RANKS * PACK, D), (64 * D) ** -0.5, 0.01171875, ((0, 32),)),
        "log_normalizer": gaussian(key_of[17], (RANKS * PACK,), 0.1, 0.6, ((0, 32),), jnp.float32),
    }


norm_eps = 1e-06
rope_theta = 1000000.0
clip_low = 0.2
clip_high = 0.28
std_floor = 1.0
mask_fill = -1e+30

def rotary(matrix, positions):
    half_size = matrix.shape[-1] // 2
    exponents = jnp.arange(half_size, dtype=jnp.float32) * (2.0 / matrix.shape[-1])
    frequency = rope_theta ** (-exponents)
    angles = positions[:, None] * frequency[None, :]
    cosine_table = jnp.cos(angles)[:, None, :]
    sine_table = jnp.sin(angles)[:, None, :]
    first_half = matrix[..., :half_size]
    second_half = matrix[..., half_size:]
    return jnp.concatenate([first_half * cosine_table - second_half * sine_table, second_half * cosine_table + first_half * sine_table], -1)

def reference(hidden, old_logp, rewards, resp_dest, resp_len, resp_offset, prompt_group, attn_gain, w_query, q_bias, w_key, k_bias, w_value, v_bias, w_out, final_gain, chosen_rows, log_normalizer):
    highest = lax.Precision.HIGHEST
    group_total = RESPONSES // GROUP_SIZE
    member = (prompt_group[:, None] == jnp.arange(group_total, dtype=jnp.int32)[None, :]).astype(jnp.float32)
    group_mean = jnp.dot(rewards, member, precision=highest) / GROUP_SIZE
    centered = rewards - jnp.dot(member, group_mean, precision=highest)
    spread = jnp.dot(centered * centered, member, precision=highest) / GROUP_SIZE
    group_scale = jnp.maximum(jnp.sqrt(spread), std_floor)
    advantage = centered / jnp.dot(member, group_scale, precision=highest)
    response_ids = jnp.arange(RESPONSES, dtype=jnp.int32)[None, :]
    slots = jnp.arange(PACK, dtype=jnp.int32)[:, None]

    def one_rank(dest_rank):
        covered = (resp_dest[None, :] == dest_rank) & (slots >= resp_offset[None, :]) & (slots < resp_offset[None, :] + resp_len[None, :])
        occupied = jnp.any(covered, 1)
        within_all = slots - resp_offset[None, :]
        token_index = lax.optimization_barrier(jnp.sum(jnp.where(covered, response_ids * MAXLEN + within_all, 0), 1)).astype(jnp.int32)
        positions = lax.optimization_barrier(jnp.sum(jnp.where(covered, within_all, 0), 1)).astype(jnp.float32)
        segment = jnp.where(occupied, lax.optimization_barrier(jnp.sum(jnp.where(covered, response_ids, 0), 1)), -1)
        token_adv = lax.optimization_barrier(jnp.sum(jnp.where(covered, advantage[None, :], 0.0), 1))
        packed = jnp.where(occupied[:, None], hidden[token_index], jnp.zeros((), hidden.dtype))
        wide = packed.astype(jnp.float32)
        inverse = lax.rsqrt(lax.optimization_barrier(jnp.mean(wide * wide, -1, keepdims=True)) + norm_eps)
        normed = (wide * inverse * attn_gain.astype(jnp.float32)).astype(jnp.bfloat16)
        queries = jnp.dot(normed, w_query, preferred_element_type=jnp.float32) + q_bias.astype(jnp.float32)
        queries = rotary(queries.reshape(PACK, HEADS, HEAD), positions).astype(jnp.bfloat16)
        key_rows = jnp.dot(normed, w_key, preferred_element_type=jnp.float32) + k_bias.astype(jnp.float32)
        key_rows = rotary(key_rows.reshape(PACK, KV_HEADS, HEAD), positions).astype(jnp.bfloat16)
        value_rows = (jnp.dot(normed, w_value, preferred_element_type=jnp.float32) + v_bias.astype(jnp.float32)).astype(jnp.bfloat16).reshape(PACK, KV_HEADS, HEAD)
        grouped = queries.reshape(PACK, KV_HEADS, HEADS // KV_HEADS, HEAD).astype(jnp.float32)
        scores = jnp.einsum('qkgd,ekd->kgqe', grouped, key_rows.astype(jnp.float32)) * HEAD ** (-0.5)
        order_ids = jnp.arange(PACK, dtype=jnp.int32)
        allowed = (segment[:, None] == segment[None, :]) & (order_ids[None, :] <= order_ids[:, None])
        scores = jnp.where(allowed, scores, mask_fill)
        highest_score = lax.optimization_barrier(jnp.max(scores, -1, keepdims=True))
        exponent = jnp.exp(scores - highest_score)
        weights = (exponent / lax.optimization_barrier(jnp.sum(exponent, -1, keepdims=True))).astype(jnp.bfloat16)
        mixed = jnp.einsum('kgqe,ekd->qkgd', weights.astype(jnp.float32), value_rows.astype(jnp.float32))
        mixed = mixed.reshape(PACK, HEADS * HEAD).astype(jnp.bfloat16)
        partial_value = jnp.einsum('pgx,gxd->gpd', mixed.reshape(PACK, N_MP, -1).astype(jnp.float32), w_out.reshape(N_MP, -1, D).astype(jnp.float32)).astype(jnp.bfloat16)
        branch = lax.optimization_barrier(jnp.sum(partial_value.astype(jnp.float32), 0))
        residual_out = (wide + branch).astype(jnp.bfloat16)
        final_rows = residual_out.astype(jnp.float32)
        final_inverse = lax.rsqrt(lax.optimization_barrier(jnp.mean(final_rows * final_rows, -1, keepdims=True)) + norm_eps)
        first_row = (dest_rank * PACK).astype(jnp.int32)
        chosen = lax.dynamic_slice_in_dim(chosen_rows, first_row, PACK, 0).astype(jnp.float32)
        normalizer = lax.dynamic_slice_in_dim(log_normalizer, first_row, PACK, 0)
        logits = lax.optimization_barrier(jnp.sum(final_rows * final_inverse * final_gain.astype(jnp.float32) * chosen, -1))
        old_values = jnp.where(occupied, old_logp[token_index], 0.0)
        ratios = jnp.exp(logits - normalizer - old_values)
        bounded = jnp.clip(ratios, 1.0 - clip_low, 1.0 + clip_high)
        objective = jnp.where(occupied, jnp.minimum(ratios * token_adv, bounded * token_adv), 0.0)
        return (objective, occupied.astype(jnp.float32))
    objective, counted = lax.map(one_rank, jnp.arange(RANKS, dtype=jnp.int32))
    objective = objective.reshape(-1)
    loss = -jnp.sum(objective) / jnp.sum(counted)
    return (objective, loss)
```

```python
import functools

import jax
import jax.numpy as jnp
import numpy as np
from jax import lax
from jax.experimental import pallas as pl
from jax.experimental.pallas import tpu as pltpu
from jax.sharding import PartitionSpec as P

HEAD = 128
GROUP_SIZE = 8
MESH = pl.DeviceIdType.MESH

norm_eps = 1e-06
rope_theta = 1000000.0
clip_low = 0.2
clip_high = 0.28
std_floor = 1.0
mask_fill = -1e30
VMEM = pl.BlockSpec(memory_space=pltpu.VMEM)
ANY = pl.BlockSpec(memory_space=pl.ANY)


def rank_peers(rows, cols):
    r, c = lax.axis_index("row"), lax.axis_index("col")
    return [
        {"row": lax.rem(r + i, rows), "col": lax.rem(c + j, cols)}
        for i in range(rows)
        for j in range(cols)
        if i or j
    ]


def main_kernel(
    rows,
    cols,
    hidden_hbm,
    logp,
    reward_in,
    dest_in,
    len_in,
    off_in,
    group_in,
    gain,
    wq_hbm,
    qb,
    wk_hbm,
    kb,
    wv_hbm,
    vb,
    wo_hbm,
    freq,
    normalizer,
    chosen_hbm,
    fgain,
    obj_ref,
    loss_ref,
    hidden,
    meta,
    everything,
    outgoing,
    recv,
    x,
    wq,
    wk,
    wv,
    wo,
    chosen,
    kbuf,
    vbuf,
    seg,
    pos,
    mixed,
    ptmp,
    r_comb,
    r_pair,
    r_cross,
    lsend,
    lrecv,
    lsend2,
    lrecv2,
    w_sem,
    f_send,
    f_recv,
    ex_send,
    ex_recv,
    g_send,
    g_recv,
    rs_send,
    rs_recv,
    l_send,
    l_recv,
    l2_send,
    l2_recv,
):
    me = lax.axis_index("mp")
    row = lax.axis_index("row")
    pair = me + 1 - 2 * lax.rem(me, 2)
    cross = lax.rem(me + 2, 4)
    diag = lax.rem(pair + 2, 4)
    mp_peers = (pair, cross, diag)
    peers = rank_peers(rows, cols)
    pack, width = x.shape
    feats = hidden.shape[1]
    count, slot = logp.shape
    blocks = width // feats
    chunk = pack // blocks
    heads = wq.shape[1] // HEAD

    load = pltpu.make_async_copy(hidden_hbm, hidden, w_sem.at[5])
    load.start()
    weights = [
        pltpu.make_async_copy(src, dst, w_sem.at[i])
        for i, (src, dst) in enumerate(
            ((wq_hbm, wq), (wk_hbm, wk), (wv_hbm, wv), (wo_hbm, wo), (chosen_hbm, chosen))
        )
    ]
    for copy in weights:
        copy.start()

    def iota(shape, dim):
        return lax.broadcasted_iota(jnp.int32, shape, dim)

    def upright(line):
        n = line.shape[1]
        return jnp.sum(jnp.where(iota((n, n), 0) == iota((n, n), 1), line, 0.0), 1, keepdims=True)

    def flat_of(column):
        n = column.shape[0]
        return jnp.sum(jnp.where(iota((n, n), 0) == iota((n, n), 1), column, 0.0), 0, keepdims=True)

    facts = [
        upright(ref[...].astype(jnp.float32))
        for ref in (reward_in, dest_in, len_in, off_in, group_in)
    ]
    tile = jnp.zeros((count, 128), jnp.float32)
    for i, fact in enumerate(facts):
        tile = jnp.where(iota(tile.shape, 1) == i, fact, tile)
    meta[:, 0:slot] = logp[...]
    meta[:, slot : slot + 128] = tile

    barrier = pltpu.get_barrier_semaphore()
    for peer in peers:
        pl.semaphore_signal(barrier, inc=1, device_id=peer, device_id_type=MESH)
    for peer in mp_peers:
        pl.semaphore_signal(barrier, inc=1, device_id={"mp": peer}, device_id_type=MESH)
    pl.semaphore_wait(barrier, len(peers) + len(mp_peers))

    def span(c):
        return pl.ds(pl.multiple_of(c * chunk, chunk), chunk)

    def lanes(d):
        return pl.ds(pl.multiple_of(d * feats, 128), feats)

    def exchange(k, c):
        return pltpu.make_async_remote_copy(
            src_ref=outgoing.at[k - 1, span(c)],
            dst_ref=recv.at[k - 1, span(c)],
            send_sem=ex_send.at[k - 1, c],
            recv_sem=ex_recv.at[k - 1, c],
            device_id={"row": lax.rem(row + k, rows)},
            device_id_type=MESH,
        )

    shared = []
    for k, peer in enumerate(peers):
        copy = pltpu.make_async_remote_copy(
            src_ref=meta,
            dst_ref=everything.at[k + 1],
            send_sem=f_send.at[k],
            recv_sem=f_recv.at[k],
            device_id=peer,
            device_id_type=MESH,
        )
        copy.start()
        shared.append(copy)
    everything[0] = meta[...]
    load.wait()
    column = lax.axis_index("col")
    _, dest, length, offset, _ = facts

    def packed(k, c):
        to = (lax.rem(row + k, rows) * cols + column).astype(jnp.float32)
        within = (c * chunk + iota((count, chunk), 1)).astype(jnp.float32) - offset
        hit = (dest == to) & (within >= 0.0) & (within < length)
        base = (iota((count, chunk), 0) * slot + 1).astype(jnp.float32)
        source = jnp.sum(jnp.where(hit, base + within, 0.0), 0, keepdims=True) - 1.0
        source = upright(source).astype(jnp.int32)
        chooser = jnp.where(iota((chunk, count * slot), 1) == source, 1.0, 0.0)
        return jnp.dot(
            chooser.astype(jnp.bfloat16), hidden[...], preferred_element_type=jnp.float32
        ).astype(jnp.bfloat16)

    def pack_out(c, carry):
        for k in range(1, rows):
            outgoing[k - 1, span(c), :] = packed(k, c)

            @pl.when(c == 0)
            def _():
                exchange(k, c).start()

        return carry

    def pack_own(c, carry):
        x[span(c), lanes(me)] = packed(0, c)
        return carry

    lax.fori_loop(0, blocks, pack_out, 0)
    lax.fori_loop(0, blocks, pack_own, 0)

    for copy in shared:
        copy.wait_recv()
    total_count = rows * cols * count
    table = everything[...].reshape(total_count, slot + 128)
    reward, dest, length, offset, group = (table[:, slot + i : slot + i + 1] for i in range(5))
    same = jnp.where(group == flat_of(group), 1.0, 0.0)
    centered = reward - jnp.sum(same * flat_of(reward), 1, keepdims=True) / GROUP_SIZE
    spread = flat_of(centered)
    spread = jnp.sum(same * (spread * spread), 1, keepdims=True) / GROUP_SIZE
    advantage = centered / jnp.maximum(jnp.sqrt(spread), std_floor)
    rank = (row * cols + column).astype(jnp.float32)

    def cover(first, size):
        within = (first + iota((total_count, size), 1)).astype(jnp.float32) - offset
        return (dest == rank) & (within >= 0.0) & (within < length), within

    covered, within = cover(me * chunk, chunk)
    token = jnp.sum(jnp.where(covered, within, 0.0), 0, keepdims=True)
    mine = jnp.where(covered, 1.0, 0.0)
    adv = jnp.sum(jnp.where(covered, advantage, 0.0), 0, keepdims=True)
    occupied = jnp.sum(mine, 0, keepdims=True)
    olds = lax.dot_general(
        table[:, :slot],
        mine,
        (((0,), (0,)), ((), ())),
        precision=lax.Precision.HIGHEST,
        preferred_element_type=jnp.float32,
    )
    old = jnp.sum(
        jnp.where(iota(olds.shape, 0).astype(jnp.float32) == token, olds, 0.0), 0, keepdims=True
    )
    counted = jnp.sum(jnp.broadcast_to(length, (total_count, chunk)), 0, keepdims=True)
    covered, within = cover(0, pack)
    which = (iota((total_count, pack), 0) + 1).astype(jnp.float32)
    seg[:, chunk : chunk + pack] = jnp.sum(jnp.where(covered, which, 0.0), 0, keepdims=True)
    seg[:, 0:chunk] = jnp.full((1, chunk), -1.0, jnp.float32)
    pos[...] = jnp.sum(jnp.where(covered, within, 0.0), 0, keepdims=True)

    def gather(kind, c):
        owner = cross if kind == 2 else me
        place = x.at[span(c), lanes(owner)]
        return pltpu.make_async_remote_copy(
            src_ref=place,
            dst_ref=place,
            send_sem=g_send.at[kind, c],
            recv_sem=g_recv.at[kind, c],
            device_id={"mp": cross if kind == 1 else pair},
            device_id_type=MESH,
        )

    def gathered(kind, c):
        owner = (pair, cross, diag)[kind]
        place = x.at[span(c), lanes(owner)]
        return pltpu.make_async_remote_copy(
            src_ref=place,
            dst_ref=place,
            send_sem=g_send.at[kind, c],
            recv_sem=g_recv.at[kind, c],
            device_id={"mp": cross if kind == 1 else pair},
            device_id_type=MESH,
        )

    def stage_a(c):
        for k in range(1, rows):
            exchange(k, c).wait()

            @pl.when(c + 1 < blocks)
            def _():
                exchange(k, c + 1).start()

        total = x[span(c), lanes(me)]
        for k in range(1, rows):
            total = total + recv[k - 1, span(c), :]
        x[span(c), lanes(me)] = total
        gather(1, c).start()
        gather(0, c).start()

    def scatter(kind, c, s):
        target = (r_comb, r_pair, r_cross)[kind]
        return pltpu.make_async_remote_copy(
            src_ref=ptmp.at[c, :, pl.ds(s * feats, feats)],
            dst_ref=target.at[:, pl.ds(s * feats, feats)],
            send_sem=rs_send.at[kind, s],
            recv_sem=rs_recv.at[kind, s],
            device_id={"mp": cross if kind == 2 else pair},
            device_id_type=MESH,
        )

    kbuf[0:chunk, :] = jnp.zeros((chunk, HEAD), kbuf.dtype)
    vbuf[0:chunk, :] = jnp.zeros((chunk, HEAD), vbuf.dtype)
    stage_a(0)
    for copy in weights:
        copy.wait()

    def step(c, carry):
        @pl.when(c + 1 < blocks)
        def _():
            stage_a(c + 1)

        gathered(1, c).wait_recv()
        gather(2, c).start()
        gathered(0, c).wait_recv()
        gathered(2, c).wait_recv()
        wide = x[span(c), :].astype(jnp.float32)
        inverse = lax.rsqrt(jnp.mean(wide * wide, -1, keepdims=True) + norm_eps)
        normed = (wide * inverse * gain[...].astype(jnp.float32)).astype(jnp.bfloat16)
        angles = upright(pos[:, span(c)]) * freq[...]
        cos_c, sin_c = jnp.cos(angles), jnp.sin(angles)
        sin_c = jnp.where(iota(angles.shape, 1) < HEAD // 2, -sin_c, sin_c)

        def rope(value):
            return (value * cos_c + pltpu.roll(value, HEAD // 2, 1) * sin_c).astype(jnp.bfloat16)

        after = pl.ds(pl.multiple_of((c + 1) * chunk, chunk), chunk)
        window = pl.ds(pl.multiple_of(c * chunk, chunk), 2 * chunk)
        key = jnp.dot(normed, wk[...], preferred_element_type=jnp.float32)
        kbuf[after, :] = rope(key + kb[...].astype(jnp.float32))
        value = jnp.dot(normed, wv[...], preferred_element_type=jnp.float32)
        vbuf[after, :] = (value + vb[...].astype(jnp.float32)).astype(jnp.bfloat16)
        query = jnp.dot(normed, wq[...], preferred_element_type=jnp.float32)
        query = query + qb[...].astype(jnp.float32)
        keys, values = kbuf[window, :], vbuf[window, :]
        shape = (chunk, 2 * chunk)
        allowed = (upright(seg[:, after]) == seg[:, window]) & (
            lax.broadcasted_iota(jnp.int32, shape, 1)
            <= lax.broadcasted_iota(jnp.int32, shape, 0) + chunk
        )
        for h in range(heads):
            cut = slice(h * HEAD, (h + 1) * HEAD)
            scores = lax.dot_general(
                rope(query[:, cut]),
                keys,
                (((1,), (1,)), ((), ())),
                preferred_element_type=jnp.float32,
            ) * HEAD ** (-0.5)
            scores = jnp.where(allowed, scores, mask_fill)
            exponent = jnp.exp(scores - jnp.max(scores, -1, keepdims=True))
            share = (exponent / jnp.sum(exponent, -1, keepdims=True)).astype(jnp.bfloat16)
            mixed[:, cut] = jnp.dot(share, values, preferred_element_type=jnp.float32).astype(
                jnp.bfloat16
            )
        for s in range(blocks):
            cut = slice(s * feats, (s + 1) * feats)
            ptmp[c, :, cut] = jnp.dot(
                mixed[...], wo[:, cut], preferred_element_type=jnp.float32
            ).astype(jnp.bfloat16)

            @pl.when(c == diag)
            def _():
                scatter(0, c, s).start()

            @pl.when(c == pair)
            def _():
                scatter(1, c, s).start()

        @pl.when(c == cross)
        def _():
            for s in range(blocks):
                cut = slice(s * feats, (s + 1) * feats)
                scatter(0, c, s).wait_recv()
                ptmp[c, :, cut] = (
                    ptmp[c, :, cut].astype(jnp.float32) + r_comb[:, cut].astype(jnp.float32)
                ).astype(jnp.bfloat16)
                scatter(2, c, s).start()

        return carry

    lax.fori_loop(0, blocks, step, 0)

    squares = jnp.zeros((chunk, 1), jnp.float32)
    product = jnp.zeros((chunk, 1), jnp.float32)
    for s in range(blocks):
        cut = slice(s * feats, (s + 1) * feats)
        scatter(1, me, s).wait_recv()
        scatter(2, me, s).wait_recv()
        branch = (
            ptmp[me, :, cut].astype(jnp.float32)
            + r_pair[:, cut].astype(jnp.float32)
            + r_cross[:, cut].astype(jnp.float32)
        )
        final = (x[span(me), cut].astype(jnp.float32) + branch).astype(jnp.bfloat16)
        final = final.astype(jnp.float32)
        squares = squares + jnp.sum(final * final, -1, keepdims=True)
        product = product + jnp.sum(
            final * fgain[:, cut].astype(jnp.float32) * chosen[:, cut].astype(jnp.float32),
            -1,
            keepdims=True,
        )
    logits = product * lax.rsqrt(squares / width + norm_eps)
    eye = lax.broadcasted_iota(jnp.int32, (chunk, chunk), 0) == lax.broadcasted_iota(
        jnp.int32, (chunk, chunk), 1
    )
    logits = jnp.sum(jnp.where(eye, logits, 0.0), 0, keepdims=True)
    ratios = jnp.exp(logits - normalizer[...] - old)
    bounded = jnp.clip(ratios, 1.0 - clip_low, 1.0 + clip_high)
    objective = jnp.where(occupied > 0.5, jnp.minimum(ratios * adv, bounded * adv), 0.0)
    obj_ref[...] = objective

    total = jnp.broadcast_to(jnp.sum(objective, -1, keepdims=True), lsend.shape)
    lsend[...] = total
    lrecv[me] = total
    copies = []
    for k, peer in enumerate(mp_peers):
        copy = pltpu.make_async_remote_copy(
            src_ref=lsend,
            dst_ref=lrecv.at[me],
            send_sem=l_send.at[k],
            recv_sem=l_recv.at[k],
            device_id={"mp": peer},
            device_id_type=MESH,
        )
        copy.start()
        copies.append(copy)
    for copy in shared:
        copy.wait_send()
    for c in range(blocks):
        for kind in range(3):
            gather(kind, c).wait_send()
    for s in range(blocks):
        scatter(0, diag, s).wait_send()
        scatter(1, pair, s).wait_send()
        scatter(2, cross, s).wait_send()
    for copy in copies:
        copy.wait()
    rank = row * cols + column
    total = lrecv[0]
    for k in range(1, blocks):
        total = total + lrecv[k]
    lsend2[...] = total
    lrecv2[rank] = total
    copies = []
    for k, peer in enumerate(peers):
        copy = pltpu.make_async_remote_copy(
            src_ref=lsend2,
            dst_ref=lrecv2.at[rank],
            send_sem=l2_send.at[k],
            recv_sem=l2_recv.at[k],
            device_id=peer,
            device_id_type=MESH,
        )
        copy.start()
        copies.append(copy)
    for copy in copies:
        copy.wait()
    total = lrecv2[0]
    for k in range(1, rows * cols):
        total = total + lrecv2[k]
    loss_ref[...] = -total[0:1, :] / counted


def body(
    hidden,
    old_logp,
    rewards,
    resp_dest,
    resp_len,
    resp_offset,
    prompt_group,
    attn_gain,
    w_query,
    q_bias,
    w_key,
    k_bias,
    w_value,
    v_bias,
    w_out,
    final_gain,
    chosen_rows,
    log_normalizer,
):
    rows, cols, mp = lax.axis_size("row"), lax.axis_size("col"), lax.axis_size("mp")
    ranks = rows * cols
    count = resp_dest.shape[0]
    slot, feats = hidden.shape[0] // count, hidden.shape[1]
    own_rows, width = chosen_rows.shape
    pack = own_rows * mp
    half = np.arange(HEAD, dtype=np.float32) % (HEAD // 2)
    freq = np.float32(rope_theta) ** (-(half * np.float32(2.0 / HEAD)))
    freq = freq.astype(np.float32)[None, :]
    dma = pltpu.SemaphoreType.DMA
    bf16, f32 = jnp.bfloat16, jnp.float32
    objective, loss = pl.pallas_call(
        functools.partial(main_kernel, rows, cols),
        out_shape=(
            jax.ShapeDtypeStruct((1, own_rows), f32),
            jax.ShapeDtypeStruct((1, own_rows), f32),
        ),
        in_specs=[ANY]
        + [VMEM] * 7
        + [ANY, VMEM, ANY, VMEM, ANY, VMEM, ANY, VMEM, VMEM, ANY, VMEM],
        out_specs=(VMEM, VMEM),
        scratch_shapes=[
            pltpu.VMEM(hidden.shape, bf16),
            pltpu.VMEM((count, slot + 128), f32),
            pltpu.VMEM((ranks, count, slot + 128), f32),
            pltpu.VMEM((max(rows - 1, 1), pack, feats), bf16),
            pltpu.VMEM((max(rows - 1, 1), pack, feats), bf16),
            pltpu.VMEM((pack, width), bf16),
            pltpu.VMEM(w_query.shape, bf16),
            pltpu.VMEM(w_key.shape, bf16),
            pltpu.VMEM(w_value.shape, bf16),
            pltpu.VMEM(w_out.shape, bf16),
            pltpu.VMEM(chosen_rows.shape, bf16),
            pltpu.VMEM((pack + own_rows, HEAD), bf16),
            pltpu.VMEM((pack + own_rows, HEAD), bf16),
            pltpu.VMEM((1, pack + own_rows), f32),
            pltpu.VMEM((1, pack), f32),
            pltpu.VMEM((own_rows, feats), bf16),
            pltpu.VMEM((mp, own_rows, width), bf16),
            pltpu.VMEM((own_rows, width), bf16),
            pltpu.VMEM((own_rows, width), bf16),
            pltpu.VMEM((own_rows, width), bf16),
            pltpu.VMEM((8, 128), f32),
            pltpu.VMEM((mp, 8, 128), f32),
            pltpu.VMEM((8, 128), f32),
            pltpu.VMEM((ranks, 8, 128), f32),
            dma((6,)),
            dma((ranks - 1,)),
            dma((ranks - 1,)),
            dma((max(rows - 1, 1), mp)),
            dma((max(rows - 1, 1), mp)),
            dma((3, mp)),
            dma((3, mp)),
            dma((3, mp)),
            dma((3, mp)),
            dma((mp - 1,)),
            dma((mp - 1,)),
            dma((ranks - 1,)),
            dma((ranks - 1,)),
        ],
        compiler_params=pltpu.CompilerParams(
            collective_id=0, has_side_effects=True, vmem_limit_bytes=60 * 1024 * 1024
        ),
        name="block",
    )(
        hidden,
        old_logp.reshape(count, slot),
        rewards[None, :],
        resp_dest[None, :],
        resp_len[None, :],
        resp_offset[None, :],
        prompt_group[None, :],
        attn_gain[None, :],
        w_query,
        q_bias[None, :],
        w_key,
        k_bias[None, :],
        w_value,
        v_bias[None, :],
        w_out,
        freq,
        log_normalizer[None, :],
        chosen_rows,
        final_gain[None, :],
    )
    return (objective.reshape(-1), loss[0, 0])


def solution(mesh):
    return jax.shard_map(
        body,
        mesh=mesh,
        in_specs=(
            P(("row", "col"), "mp"),
            P(("row", "col")),
            P(("row", "col")),
            P(("row", "col")),
            P(("row", "col")),
            P(("row", "col")),
            P(("row", "col")),
            P(),
            P(None, "mp"),
            P("mp"),
            P(None, "mp"),
            P("mp"),
            P(None, "mp"),
            P("mp"),
            P("mp", None),
            P(),
            P(("row", "col", "mp"), None),
            P(("row", "col", "mp")),
        ),
        out_specs=(P(("row", "col", "mp")), P()),
        check_vma=False,
    )
```
